128 devices in a mesh: wide: 32 (over z_hi, y, x), narrow: 4 (over z_lo, core).
Axes of the slice: x: 4, y: 4, z: 4 (z_hi: 2, z_lo: 2; z = z_hi * 2 + z_lo), core: 2. Of those that a mesh axis runs over, the one named last changes fastest.
Arguments:
- density: float32 [256, 256, 256], P('wide', 'narrow'), may hold values from -48 to 48
Outputs:
- recon_real: float32 [256, 256, 256], P('narrow', 'wide')
- recon_imag: float32 [256, 256, 256], P('narrow', 'wide')
The draws below stay inside these ranges and needn't reach their ends.
All inputs are finite; a program needn't handle non-finite values.
Results may differ from the reference program's by a relative error of at most 0.0003.
Values sent between devices are 32-bit elements; how exact they have to be, the bound alone decides.
A program may use at most 128 MiB of HBM per device.

```python
import math
import jax
import jax.numpy as jnp

GRID = 256


def block_scale(rng, shape, split, smallest, high):
    loudness, own = 1.0, jax.random.fold_in(rng, 6)
    for position, shards_of in split:
        steps = jnp.exp(jax.random.uniform(jax.random.fold_in(own, position), (shards_of,), jnp.float32, smallest / len(split), high / len(split)))
        loudness = loudness * jnp.repeat(steps, shape[position] // shards_of).reshape([-1 if axis == position else 1 for axis in range(len(shape))])
    return loudness


def normal_values(own_key, shape, deviation, reach, cuts=(), kind=jnp.bfloat16):
    drawn = deviation * jax.random.normal(own_key, shape, jnp.float32)
    if cuts:
        drawn = drawn * block_scale(own_key, shape, cuts, -0.22, 0.18)
    return jnp.clip(drawn, -reach, reach).astype(kind)


def setup_inputs(seed: int = 0) -> dict:
    splits = jax.random.split(jax.random.key(seed), 2)
    density = normal_values(splits[0], (GRID, GRID, GRID), 8.0, 48.0, ((0, 32), (1, 4)), jnp.float32)
    return {"density": density}


def wavenumbers():
    indices = jnp.arange(GRID, dtype=jnp.int32)
    signed = jnp.where(indices < GRID // 2, indices, indices - GRID)
    return signed.astype(jnp.float32) * (2.0 * math.pi / GRID), indices != GRID // 2


def reference(density):
    spectrum = jnp.fft.fftn(density)
    wave, usable = wavenumbers()
    wave_x = wave[:, None, None]
    wave_y = wave[None, :, None]
    wave_z = wave[None, None, :]
    squared = wave_x * wave_x + wave_y * wave_y + wave_z * wave_z
    keep = usable[:, None, None] & usable[None, :, None] & usable[None, None, :] & (squared > 0)
    squared_safe = jnp.where(squared > 0, squared, jnp.ones_like(squared))
    smooth_kernel = jnp.where(keep, jnp.exp(-0.5 * squared) / squared_safe, jnp.zeros_like(squared))
    waves = [wave_x, wave_y, wave_z]
    pairs = [(0, 0), (1, 1), (2, 2), (0, 1), (0, 2), (1, 2)]
    shear = jnp.zeros(density.shape, jnp.float32)
    for number, (first, second) in enumerate(pairs):
        kernel = smooth_kernel * waves[first] * waves[second]
        tidal = jnp.real(jnp.fft.ifftn(spectrum * kernel))
        weight = 1.0 if number < 3 else 2.0
        shear = shear + weight * tidal * tidal
    recon = jnp.fft.fftn(shear) / (float(GRID) ** 1.5)
    recon = recon.at[0, 0, 0].set(0.0)
    recon_real = jnp.transpose(jnp.real(recon), (2, 1, 0)).astype(jnp.float32)
    recon_imag = jnp.transpose(jnp.imag(recon), (2, 1, 0)).astype(jnp.float32)
    return recon_real, recon_imag
```

```python
import math

import jax
import jax.numpy as jnp
import ml_dtypes
import numpy as np
from jax import lax
from jax.experimental import pallas as pl
from jax.experimental.pallas import tpu as pltpu
from jax.sharding import PartitionSpec as P

MESH = pl.DeviceIdType.MESH
BF16 = jnp.bfloat16
F32 = jnp.float32
N = 256
H = 128
STEP = 2.0 * math.pi / N
NUM = 128


def split_np(table):
    table = np.asarray(table, np.float32)
    high = table.astype(ml_dtypes.bfloat16)
    low = (table - high.astype(np.float32)).astype(ml_dtypes.bfloat16)
    return high, low


def angle(rows, cols):
    return (np.asarray(rows)[:, None] * np.asarray(cols)[None, :] % N) * STEP


def tables():
    half = np.arange(H)
    full = np.arange(N)
    slab = np.concatenate([half, [H], N - half[1:]])
    wave = half * STEP
    weight = np.where(half == 0, 1.0, 2.0) / N
    cos_sin = np.concatenate([np.cos(angle(half, full)), np.sin(angle(half, full))])

    def back(points, power):
        cosine = np.cos(angle(points, half)) * (weight * wave**power)
        sine = np.sin(angle(points, half)) * (weight * wave**power)
        if power == 1:
            return np.concatenate([sine, -cosine], axis=1)
        return np.concatenate([cosine, sine], axis=1)

    back_slab = [back(slab, power) for power in range(3)]
    back_full = [back(full, power) for power in range(3)]
    pieces = []
    for part in range(4):
        cols = 64 * part + np.arange(64)
        pieces += [np.cos(angle(full, cols)), -np.sin(angle(full, cols))]
    last_z = np.concatenate(pieces, axis=1)
    last_y = np.concatenate([np.cos(angle(full, full)), np.sin(angle(full, full))])
    even = np.cos(angle(half, full))
    odd = np.sin(angle(half, full))
    odd[0] = np.where(full % 2 == 0, 1.0, -1.0)
    last_x = np.concatenate([even, odd]) / float(N) ** 1.5
    out = []
    for table in [cos_sin] + back_slab + back_full + [last_z, last_y, last_x]:
        out += list(split_np(table))
    return out


def split(value):
    high = value.astype(BF16)
    low = (value - high.astype(F32)).astype(BF16)
    return high, low


def product(left, right, dims):
    def one(a, b):
        return lax.dot_general(a, b, (dims, ((), ())), preferred_element_type=F32)

    return one(left[0], right[0]) + (one(left[0], right[1]) + one(left[1], right[0]))


ROW_COL = ((1,), (0,))
ROW_ROW = ((1,), (1,))
COL_COL = ((0,), (0,))
PAIRS = ((0, 0, 1.0), (0, 1, 2.0), (0, 2, 1.0), (1, 0, 2.0), (1, 1, 2.0), (2, 0, 1.0))


def device(place):
    return {"wide": place // 4, "narrow": place % 4}


def body(density, *refs):
    consts, refs = refs[:20], refs[20:]
    real_out, imag_out, refs = refs[0], refs[1], refs[2:]
    (tabs, refs) = refs[:20], refs[20:]
    send1, recv1 = refs[0], refs[1]
    send2, recv2 = refs[2:5], refs[5:8]
    send3, recv3 = refs[8:10], refs[10:12]
    final = refs[12:16]
    shear_ref, load_sem, store_sem, sent, got = refs[16:]
    wide = lax.axis_index("wide")
    narrow = lax.axis_index("narrow")
    me = wide * 4 + narrow

    barrier = pltpu.get_barrier_semaphore()

    def greet(step, carry):
        pl.semaphore_signal(
            barrier, inc=1, device_id=device((me + step) % NUM), device_id_type=MESH
        )
        return carry

    lax.fori_loop(1, NUM, greet, 0)
    loads = [
        pltpu.make_async_copy(consts[i], tabs[i], load_sem.at[i]) for i in range(20)
    ]
    for load in loads:
        load.start()

    def table(number):
        return tabs[2 * number][...], tabs[2 * number + 1][...]

    def ready(number):
        loads[2 * number].wait()
        loads[2 * number + 1].wait()

    def exchange(source, target, mine_from, mine_to, phase):
        pltpu.make_async_copy(mine_from, mine_to, got.at[phase]).start()

        def start(step, carry):
            place = (me + step * 37) % NUM
            pltpu.make_async_remote_copy(
                src_ref=source(place),
                dst_ref=target,
                send_sem=sent.at[phase],
                recv_sem=got.at[phase],
                device_id=device(place),
                device_id_type=MESH,
            ).start()
            return carry

        lax.fori_loop(1, NUM, start, 0)

    def rows(ref, place):
        return ref.at[pl.ds(pl.multiple_of(place * 8, 8), 8)]

    ready(0)
    block = split(density[...].reshape(512, N))
    lines = product(table(0), block, ROW_ROW)
    for x in range(8):
        send1[pl.ds(x, H, stride=8), :] = jnp.concatenate(
            [lines[:H, 64 * x : 64 * x + 64], lines[H:, 64 * x : 64 * x + 64]], axis=1
        )
    pl.semaphore_wait(barrier, NUM - 1)
    landing = recv1.at[wide, pl.ds(pl.multiple_of(narrow * 8, 8), 8)]
    exchange(lambda place: rows(send1, place), landing, rows(send1, me), landing, 0)

    for number in range(1, 10):
        ready(number)
    wave_a = lax.broadcasted_iota(jnp.int32, (H, H), 0).astype(F32) * STEP
    wave_b = lax.broadcasted_iota(jnp.int32, (H, H), 1).astype(F32) * STEP
    wave_c = me.astype(F32) * STEP
    squared = wave_a * wave_a + wave_b * wave_b + wave_c * wave_c
    smooth = jnp.where(
        squared > 0, jnp.exp(-0.5 * squared) / jnp.where(squared > 0, squared, 1.0), 0.0
    )
    smooth = jnp.concatenate([smooth, smooth], axis=0)
    smooth = jnp.concatenate([smooth] * 4, axis=1)

    pltpu.make_async_copy(recv1, recv1, got.at[0]).wait()
    quarter = [recv1[:, 8 * n : 8 * n + 8, :].reshape(N, H) for n in range(4)]
    plane = jnp.concatenate(
        [q[:, :64] for q in quarter] + [q[:, 64:] for q in quarter], axis=1
    )
    along_x = product(table(0), split(plane), ROW_COL)
    along_x = jnp.concatenate([along_x[:, :N], along_x[:, N:]], axis=0)
    along_y = product(split(along_x), table(0), ROW_ROW)
    spectrum = jnp.concatenate([along_y[:N], along_y[N:]], axis=1)
    filtered = split(spectrum * smooth)
    for power in range(3):
        field = product(table(1 + power), filtered, ROW_COL)
        for x1 in range(2):
            for kind in range(4):
                send2[power][pl.ds(4 * x1 + kind, H, stride=8), :] = field[
                    H * x1 : H * x1 + H, H * kind : H * kind + H
                ]
        exchange(
            lambda place, power=power: rows(send2[power], place),
            rows(recv2[power], me),
            rows(send2[power], me),
            rows(recv2[power], me),
            1 + power,
        )

    for power in range(3):
        pltpu.make_async_copy(recv2[power], recv2[power], got.at[1 + power]).wait()
        for x1 in range(2):
            kinds = [recv2[power][pl.ds(4 * x1 + kind, H, stride=8), :] for kind in range(4)]
            held = jnp.concatenate(
                [
                    jnp.concatenate([kinds[0], kinds[1]], axis=1),
                    jnp.concatenate([kinds[2], kinds[3]], axis=1),
                ],
                axis=0,
            )
            held = split(held)
            total = None
            for first, second, weight in PAIRS:
                if first != power:
                    continue
                part = product(held, table(4 + second), ROW_ROW)
                tidal = product(table(4 + 2 - first - second), split(part), ROW_COL)
                term = weight * (tidal * tidal)
                total = term if total is None else total + term
            if power == 0:
                shear_ref[x1] = total
            else:
                shear_ref[x1] = shear_ref[x1] + total

    for x1 in range(2):
        lines = product(split(shear_ref[x1]), table(7), COL_COL)
        both = product(table(8), split(lines), ROW_COL)
        for n in range(4):
            swapped = pltpu.roll(both[N:, H * n : H * n + H], 64, 1)
            lane = lax.broadcasted_iota(jnp.int32, (N, H), 1)
            send3[x1][:, H * n : H * n + H] = both[:N, H * n : H * n + H] + jnp.where(
                lane < 64, swapped, -swapped
            )

        def tile(place, x1=x1):
            return send3[x1].at[
                pl.ds(pl.multiple_of(place // 4 * 8, 8), 8),
                pl.ds(pl.multiple_of(place % 4 * H, H), H),
            ]

        exchange(tile, rows(recv3[x1], me), tile(me), rows(recv3[x1], me), 4 + x1)

    for x1 in range(2):
        pltpu.make_async_copy(recv3[x1], recv3[x1], got.at[4 + x1]).wait()
    line = lax.broadcasted_iota(jnp.int32, (H, H), 0)
    lane = lax.broadcasted_iota(jnp.int32, (H, H), 1)
    for b in range(8):
        plus = recv3[0][pl.ds(b, H, stride=8), :]
        minus = recv3[1][pl.ds(b, H, stride=8), :]
        even = jnp.where(line == 0, plus, plus + minus)
        odd = plus - minus
        swapped = pltpu.roll(odd, 64, 1)
        odd = jnp.where(line == 0, minus, jnp.where(lane < 64, swapped, -swapped))
        both = jnp.concatenate([even, odd], axis=0)
        done = product(split(both), table(9), COL_COL)
        real_part, imag_part = done[:64], done[64:]
        if b == 0:
            anchor = (
                (lax.broadcasted_iota(jnp.int32, (64, N), 0) == 0)
                & (lax.broadcasted_iota(jnp.int32, (64, N), 1) == 0)
                & (me == 0)
            )
            real_part = jnp.where(anchor, 0.0, real_part)
            imag_part = jnp.where(anchor, 0.0, imag_part)
        for part, value in enumerate((real_part, imag_part)):
            for side in range(2):
                final[2 * part + side][pl.ds(b, 64, stride=8), :] = value[
                    :, H * side : H * side + H
                ]
    stores = [
        pltpu.make_async_copy(
            final[2 * part + side],
            (real_out, imag_out)[part].at[:, pl.ds(H * side, H)],
            store_sem.at[2 * part + side],
        )
        for part in range(2)
        for side in range(2)
    ]
    for store in stores:
        store.start()

    for phase, ref in enumerate([send1] + list(send2) + list(recv3)):
        part = ref.at[pl.ds(0, 8 * (NUM - 1))]
        pltpu.make_async_copy(part, part, sent.at[phase]).wait()
    for store in stores:
        store.wait()


def per_device(density):
    arrays = [jnp.asarray(table) for table in tables()]
    buffer = pltpu.VMEM((8 * NUM, H), F32)
    result = jax.ShapeDtypeStruct((512, N), F32)
    real_part, imag_part = pl.pallas_call(
        body,
        out_shape=(result, result),
        in_specs=[pl.BlockSpec(memory_space=pltpu.VMEM)]
        + [pl.BlockSpec(memory_space=pl.ANY)] * 20,
        out_specs=[pl.BlockSpec(memory_space=pl.ANY)] * 2,
        scratch_shapes=[pltpu.VMEM(array.shape, BF16) for array in arrays]
        + [buffer, pltpu.VMEM((32, 32, H), F32)]
        + [buffer] * 6
        + [pltpu.VMEM((N, 512), F32)] * 2
        + [buffer] * 2
        + [pltpu.VMEM((512, H), F32)] * 4
        + [
            pltpu.VMEM((2, N, N), F32),
            pltpu.SemaphoreType.DMA((20,)),
            pltpu.SemaphoreType.DMA((4,)),
            pltpu.SemaphoreType.DMA((6,)),
            pltpu.SemaphoreType.DMA((6,)),
        ],
        compiler_params=pltpu.CompilerParams(
            collective_id=0, has_side_effects=True, vmem_limit_bytes=56 * 2**20
        ),
        name="tidal",
    )(density, *arrays)
    return real_part.reshape(64, 8, N), imag_part.reshape(64, 8, N)


def solution(mesh):
    return jax.shard_map(
        per_device,
        mesh=mesh,
        in_specs=(P("wide", "narrow", None),),
        out_specs=(P("narrow", "wide", None), P("narrow", "wide", None)),
        check_vma=False,
    )
```

```python
import math

import jax
import jax.numpy as jnp
import ml_dtypes
import numpy as np
from jax import lax
from jax.experimental import pallas as pl
from jax.experimental.pallas import tpu as pltpu
from jax.sharding import PartitionSpec as P

LOGICAL = pl.DeviceIdType.LOGICAL
BF16 = jnp.bfloat16
F32 = jnp.float32
N = 256
H = 128
STEP = 2.0 * math.pi / N
NUM = 128


def split_np(table):
    table = np.asarray(table, np.float32)
    high = table.astype(ml_dtypes.bfloat16)
    low = (table - high.astype(np.float32)).astype(ml_dtypes.bfloat16)
    return high, low


def angle(rows, cols):
    return (np.asarray(rows)[:, None] * np.asarray(cols)[None, :] % N) * STEP


def tables():
    half = np.arange(H)
    full = np.arange(N)
    slab = np.concatenate([half, [H], N - half[1:]])
    wave = half * STEP
    weight = np.where(half == 0, 1.0, 2.0) / N
    cos_sin = np.concatenate([np.cos(angle(half, full)), np.sin(angle(half, full))])

    def back(points, power):
        cosine = np.cos(angle(points, half)) * (weight * wave**power)
        sine = np.sin(angle(points, half)) * (weight * wave**power)
        if power == 1:
            return np.concatenate([sine, -cosine], axis=1)
        return np.concatenate([cosine, sine], axis=1)

    back_slab = [back(slab, power) for power in range(3)]
    back_full = [back(full, power) for power in range(3)]
    even = np.cos(angle(half, full))
    odd = np.sin(angle(half, full))
    odd[0] = np.where(full % 2 == 0, 1.0, -1.0)
    last_x = np.concatenate([even, odd]) / float(N) ** 1.5
    order = (
        np.arange(2)[:, None, None]
        + 2 * np.arange(4)[None, :, None]
        + 8 * np.arange(32)[None, None, :]
    ).reshape(-1)
    out = []
    for table in [cos_sin, cos_sin[:, order]] + back_slab + back_full + [last_x]:
        out += list(split_np(table))
    return out


def split(value):
    high = value.astype(BF16)
    low = (value - high.astype(F32)).astype(BF16)
    return high, low


def product(left, right, dims):
    def one(a, b):
        return lax.dot_general(a, b, (dims, ((), ())), preferred_element_type=F32)

    return one(left[0], right[0]) + (one(left[0], right[1]) + one(left[1], right[0]))


ROW_COL = ((1,), (0,))
ROW_ROW = ((1,), (1,))
PAIRS = ((0, 0, 1.0), (0, 1, 2.0), (0, 2, 1.0), (1, 0, 2.0), (1, 1, 2.0), (2, 0, 1.0))


def walk(me, visit):
    def step(_, place):
        place = place + 37
        place = jnp.where(place >= NUM, place - NUM, place)
        visit(place)
        return place

    lax.fori_loop(1, NUM, step, me, unroll=8)


TABLES = 18
PHASES = 9


def body(density, *refs):
    consts, refs = refs[:TABLES], refs[TABLES:]
    real_out, imag_out, refs = refs[0], refs[1], refs[2:]
    tabs, refs = refs[:TABLES], refs[TABLES:]
    send1, recv1 = refs[0], refs[1]
    send2, recv2 = refs[2:6], refs[6:10]
    send3, recv3 = refs[10:12], refs[12:14]
    final = refs[14:18]
    load_sem, store_sem, sent, got = refs[18:]
    wide = lax.axis_index("wide")
    narrow = lax.axis_index("narrow")
    me = wide * 4 + narrow

    barrier = pltpu.get_barrier_semaphore()

    def greet(place):
        pl.semaphore_signal(barrier, inc=1, device_id=place, device_id_type=LOGICAL)

    walk(me, greet)
    loads = [
        pltpu.make_async_copy(consts[i], tabs[i], load_sem.at[i]) for i in range(TABLES)
    ]
    for load in loads:
        load.start()

    def table(number, *index):
        return tabs[2 * number][index or ...], tabs[2 * number + 1][index or ...]

    def ready(number):
        loads[2 * number].wait()
        loads[2 * number + 1].wait()

    waits = []

    def exchange(source, target, whole, phase):
        pltpu.make_async_copy(source(me), target(me), got.at[phase]).start()

        def start(place):
            pltpu.make_async_remote_copy(
                src_ref=source(place),
                dst_ref=target(me),
                send_sem=sent.at[phase],
                recv_sem=got.at[phase],
                device_id=place,
                device_id_type=LOGICAL,
            ).start()

        walk(me, start)
        part = whole.at[pl.ds(0, NUM - 1)]
        waits.append(pltpu.make_async_copy(part, part, sent.at[phase]))

    def swap(send, recv, first, count, phase):
        exchange(
            lambda place: send.at[place, pl.ds(first, count)],
            lambda place: recv.at[place, pl.ds(first, count)],
            send.at[:, pl.ds(first, count)],
            phase,
        )

    def arrive(recv, first, count, phase):
        part = recv.at[:, pl.ds(first, count)]
        pltpu.make_async_copy(part, part, got.at[phase]).wait()

    def flat(ref):
        return ref.reshape(8 * NUM, H)

    ready(0)
    block = split(density[...].reshape(512, N))
    for part in range(2):
        lines = product(table(0, pl.ds(H * part, H)), block, ROW_ROW)
        for q in range(4):
            flat(send1)[pl.ds(4 * part + q, H, stride=8), :] = lines[:, H * q : H * q + H]
        if part == 0:
            pl.semaphore_wait(barrier, NUM - 1)
        swap(send1, recv1, 4 * part, 4, part)

    for number in range(1, TABLES // 2):
        ready(number)
    wave_a = lax.broadcasted_iota(jnp.int32, (H, H), 0).astype(F32) * STEP
    wave_b = lax.broadcasted_iota(jnp.int32, (H, H), 1).astype(F32) * STEP
    wave_c = me.astype(F32) * STEP
    squared = wave_a * wave_a + wave_b * wave_b + wave_c * wave_c
    smooth = jnp.where(
        squared > 0, jnp.exp(-0.5 * squared) / jnp.where(squared > 0, squared, 1.0), 0.0
    )
    smooth = jnp.concatenate([smooth, smooth], axis=0)
    smooth = jnp.concatenate([smooth, smooth], axis=1)

    def back_x(filtered, part, x1):
        for power in range(3):
            field = product(table(2 + power, pl.ds(H * x1, H)), filtered, ROW_COL)
            for s in range(2):
                if x1 == 0:
                    ref, row = send2[part], 2 * power + s
                else:
                    ref, row = send2[2 + power // 2], 4 * (power % 2) + 2 * part + s
                flat(ref)[pl.ds(row, H, stride=8), :] = field[:, H * s : H * s + H]

    kept = []
    for part in range(2):
        arrive(recv1, 4 * part, 4, part)
        pieces = []
        for n in range(4):
            pieces.append(
                jnp.concatenate(
                    [
                        flat(recv1)[pl.ds(8 * n + 4 * part + q, 32, stride=32), :]
                        for q in range(4)
                    ],
                    axis=0,
                )
            )
        plane = jnp.concatenate(
            [
                jnp.concatenate([piece[:, 64 * low : 64 * low + 64] for piece in pieces], axis=1)
                for low in range(2)
            ],
            axis=0,
        )
        along_x = product(table(1), split(plane), ROW_COL)
        along_y = product(split(along_x), table(0), ROW_ROW)
        filtered = split(along_y * smooth)
        kept.append(filtered)
        back_x(filtered, part, 0)
        swap(send2[part], recv2[part], 0, 6, 2 + part)
    for part in range(2):
        back_x(kept[part], part, 1)
    for power in range(3):
        swap(send2[2 + power // 2], recv2[2 + power // 2], 4 * (power % 2), 4, 4 + power)

    flip_lane = 1.0 - 2.0 * (lax.broadcasted_iota(jnp.int32, (1, N), 1) & 1).astype(F32)
    flip_line = 1.0 - 2.0 * (lax.broadcasted_iota(jnp.int32, (N, 1), 0) & 1).astype(F32)

    for x1 in range(2):
        if x1 == 0:
            arrive(recv2[0], 0, 6, 2)
            arrive(recv2[1], 0, 6, 3)
        shear = None
        for power in range(3):
            if x1 == 1:
                arrive(recv2[2 + power // 2], 4 * (power % 2), 4, 4 + power)
            halves = []
            for part in range(2):
                if x1 == 0:
                    ref, row = recv2[part], 2 * power
                else:
                    ref, row = recv2[2 + power // 2], 4 * (power % 2) + 2 * part
                halves.append(
                    jnp.concatenate(
                        [flat(ref)[pl.ds(row + s, H, stride=8), :] for s in range(2)], axis=1
                    )
                )
            held = split(jnp.concatenate(halves, axis=0))
            for first, second, weight in PAIRS:
                if first != power:
                    continue
                back_y = product(held, table(5 + second), ROW_ROW)
                tidal = product(table(5 + 2 - first - second), split(back_y), ROW_COL)
                term = weight * (tidal * tidal)
                shear = term if shear is None else shear + term
        turned = jnp.transpose(shear)
        lines = []
        for high in range(2):
            lines.append(product(split(turned), table(0), ROW_ROW))
            turned = turned * flip_lane
        lines = jnp.concatenate(lines, axis=1)
        for high in range(2):
            both = product(table(0), split(lines), ROW_COL)
            lines = lines * flip_line
            for side in range(2):
                cosine = both[:H, N * side : N * side + N]
                sine = both[H:, N * side : N * side + N]
                real_part = cosine[:, :H] - sine[:, H:]
                imag_part = -(cosine[:, H:] + sine[:, :H])
                for n in range(2):
                    here = slice(64 * n, 64 * n + 64)
                    send3[x1][H * high : H * high + H, pl.ds(N * side + H * n, H)] = (
                        jnp.concatenate([real_part[:, here], imag_part[:, here]], axis=1)
                    )

        def tile(place, x1=x1):
            return send3[x1].at[
                pl.ds(pl.multiple_of(place // 4 * 8, 8), 8),
                pl.ds(pl.multiple_of(place % 4 * H, H), H),
            ]

        exchange(tile, lambda place, x1=x1: recv3[x1].at[place], recv3[x1], 7 + x1)

    arrive(recv3[0], 0, 8, 7)
    arrive(recv3[1], 0, 8, 8)
    line = lax.broadcasted_iota(jnp.int32, (H, H), 0)
    lane = lax.broadcasted_iota(jnp.int32, (H, H), 1)
    for b in range(8):
        plus = flat(recv3[0])[pl.ds(b, H, stride=8), :]
        minus = flat(recv3[1])[pl.ds(b, H, stride=8), :]
        even = jnp.where(line == 0, plus, plus + minus)
        odd = plus - minus
        swapped = pltpu.roll(odd, 64, 1)
        odd = jnp.where(line == 0, minus, jnp.where(lane < 64, swapped, -swapped))
        both = jnp.concatenate([even, odd], axis=0)
        done = product(split(jnp.transpose(both)), table(8), ROW_COL)
        real_part, imag_part = done[:64], done[64:]
        if b == 0:
            anchor = (
                (lax.broadcasted_iota(jnp.int32, (64, N), 0) == 0)
                & (lax.broadcasted_iota(jnp.int32, (64, N), 1) == 0)
                & (me == 0)
            )
            real_part = jnp.where(anchor, 0.0, real_part)
            imag_part = jnp.where(anchor, 0.0, imag_part)
        for part, value in enumerate((real_part, imag_part)):
            for side in range(2):
                final[2 * part + side][pl.ds(b, 64, stride=8), :] = value[
                    :, H * side : H * side + H
                ]
    stores = [
        pltpu.make_async_copy(
            final[2 * part + side],
            (real_out, imag_out)[part].at[:, pl.ds(H * side, H)],
            store_sem.at[2 * part + side],
        )
        for part in range(2)
        for side in range(2)
    ]
    for store in stores:
        store.start()
    for wait in waits:
        wait.wait()
    for store in stores:
        store.wait()


def per_device(density):
    arrays = [jnp.asarray(table) for table in tables()]
    buffer = pltpu.VMEM((NUM, 8, H), F32)
    result = jax.ShapeDtypeStruct((512, N), F32)
    real_part, imag_part = pl.pallas_call(
        body,
        out_shape=(result, result),
        in_specs=[pl.BlockSpec(memory_space=pltpu.VMEM)]
        + [pl.BlockSpec(memory_space=pl.ANY)] * TABLES,
        out_specs=[pl.BlockSpec(memory_space=pl.ANY)] * 2,
        scratch_shapes=[pltpu.VMEM(array.shape, BF16) for array in arrays]
        + [buffer] * 10
        + [pltpu.VMEM((N, 512), F32)] * 2
        + [buffer] * 2
        + [pltpu.VMEM((512, H), F32)] * 4
        + [
            pltpu.SemaphoreType.DMA((TABLES,)),
            pltpu.SemaphoreType.DMA((4,)),
            pltpu.SemaphoreType.DMA((PHASES,)),
            pltpu.SemaphoreType.DMA((PHASES,)),
        ],
        compiler_params=pltpu.CompilerParams(
            collective_id=0, has_side_effects=True, vmem_limit_bytes=56 * 2**20
        ),
        name="tidal",
    )(density, *arrays)
    return real_part.reshape(64, 8, N), imag_part.reshape(64, 8, N)


def solution(mesh):
    return jax.shard_map(
        per_device,
        mesh=mesh,
        in_specs=(P("wide", "narrow", None),),
        out_specs=(P("narrow", "wide", None), P("narrow", "wide", None)),
        check_vma=False,
    )
```

```python
import math

import jax
import jax.numpy as jnp
import ml_dtypes
import numpy as np
from jax import lax
from jax.experimental import pallas as pl
from jax.experimental.pallas import tpu as pltpu
from jax.sharding import PartitionSpec as P

LOGICAL = pl.DeviceIdType.LOGICAL
BF16 = jnp.bfloat16
F32 = jnp.float32
N = 256
H = 128
STEP = 2.0 * math.pi / N
NUM = 128


def split_np(table):
    table = np.asarray(table, np.float32)
    high = table.astype(ml_dtypes.bfloat16)
    low = (table - high.astype(np.float32)).astype(ml_dtypes.bfloat16)
    return high, low


def angle(rows, cols):
    return (np.asarray(rows)[:, None] * np.asarray(cols)[None, :] % N) * STEP


def tables():
    half = np.arange(H)
    full = np.arange(N)
    slab = np.concatenate([half, [H], N - half[1:]])
    wave = half * STEP
    weight = np.where(half == 0, 1.0, 2.0) / N
    cos_sin = np.concatenate([np.cos(angle(half, full)), np.sin(angle(half, full))])

    def back(points, power):
        cosine = np.cos(angle(points, half)) * (weight * wave**power)
        sine = np.sin(angle(points, half)) * (weight * wave**power)
        if power == 1:
            return np.concatenate([sine, -cosine], axis=1)
        return np.concatenate([cosine, sine], axis=1)

    back_slab = [back(slab, power) for power in range(3)]
    back_full = [back(full, power) for power in range(3)]
    even = np.cos(angle(half, full))
    odd = np.sin(angle(half, full))
    odd[0] = np.where(full % 2 == 0, 1.0, -1.0)
    last_x = np.concatenate([even, odd]) / float(N) ** 1.5
    order = (
        np.arange(2)[:, None, None]
        + 2 * np.arange(4)[None, :, None]
        + 8 * np.arange(32)[None, None, :]
    ).reshape(-1)
    out = []
    for table in [cos_sin, cos_sin[:, order]] + back_slab + back_full + [last_x]:
        out += list(split_np(table))
    return out


def split(value):
    high = value.astype(BF16)
    low = (value - high.astype(F32)).astype(BF16)
    return high, low


def product(left, right, dims):
    def one(a, b):
        return lax.dot_general(a, b, (dims, ((), ())), preferred_element_type=F32)

    return one(left[0], right[0]) + (one(left[0], right[1]) + one(left[1], right[0]))


ROW_COL = ((1,), (0,))
ROW_ROW = ((1,), (1,))
PAIRS = ((0, 0, 1.0), (0, 1, 2.0), (0, 2, 1.0), (1, 0, 2.0), (1, 1, 2.0), (2, 0, 1.0))


def walk(me, visit):
    def step(_, place):
        place = place + 37
        place = jnp.where(place >= NUM, place - NUM, place)
        visit(place)
        return place

    lax.fori_loop(1, NUM, step, me, unroll=8)


TABLES = 16
OUT = jax.ShapeDtypeStruct((NUM, 8, H), F32)
PHASES = 9


def body(density, *refs):
    consts, refs = refs[0], refs[1:]
    recv3, refs = refs[:2], refs[2:]
    tabs, refs = refs[:TABLES], refs[TABLES:]
    send1, recv1 = refs[0], refs[1]
    send2, recv2 = refs[2:6], refs[6:10]
    send3 = refs[10:12]
    field, field_sem, load_sem, sent, got = refs[12:]
    wide = lax.axis_index("wide")
    narrow = lax.axis_index("narrow")
    me = wide * 4 + narrow

    fetch = pltpu.make_async_copy(density, field, field_sem)
    fetch.start()
    barrier = pltpu.get_barrier_semaphore()

    def greet(place):
        pl.semaphore_signal(barrier, inc=1, device_id=place, device_id_type=LOGICAL)

    walk(me, greet)
    loads = [
        pltpu.make_async_copy(consts.at[pl.ds(N * i, N)], tabs[i], load_sem.at[i])
        for i in range(TABLES)
    ]
    for load in loads:
        load.start()

    def table(number, *index):
        return tabs[2 * number][index or ...], tabs[2 * number + 1][index or ...]

    def ready(number):
        loads[2 * number].wait()
        loads[2 * number + 1].wait()

    waits = []

    def exchange(source, target, whole, phase):
        pltpu.make_async_copy(source(me), target(me), got.at[phase]).start()

        def start(place):
            pltpu.make_async_remote_copy(
                src_ref=source(place),
                dst_ref=target(me),
                send_sem=sent.at[phase],
                recv_sem=got.at[phase],
                device_id=place,
                device_id_type=LOGICAL,
            ).start()

        walk(me, start)
        part = whole.at[pl.ds(0, NUM - 1)]
        waits.append(pltpu.make_async_copy(part, part, sent.at[phase]))

    def swap(send, recv, first, count, phase):
        exchange(
            lambda place: send.at[place, pl.ds(first, count)],
            lambda place: recv.at[place, pl.ds(first, count)],
            send.at[:, pl.ds(first, count)],
            phase,
        )

    def arrive(recv, first, count, phase):
        part = recv.at[:, pl.ds(first, count)]
        pltpu.make_async_copy(part, part, got.at[phase]).wait()

    def flat(ref):
        return ref.reshape(8 * NUM, H)

    ready(0)
    fetch.wait()
    block = split(field[...].reshape(512, N))
    for part in range(2):
        lines = product(table(0, pl.ds(H * part, H)), block, ROW_ROW)
        for q in range(4):
            flat(send1)[pl.ds(4 * part + q, H, stride=8), :] = lines[:, H * q : H * q + H]
        if part == 0:
            pl.semaphore_wait(barrier, NUM - 1)
        swap(send1, recv1, 4 * part, 4, part)

    for number in range(1, TABLES // 2):
        ready(number)
    wave_a = lax.broadcasted_iota(jnp.int32, (H, H), 0).astype(F32) * STEP
    wave_b = lax.broadcasted_iota(jnp.int32, (H, H), 1).astype(F32) * STEP
    wave_c = me.astype(F32) * STEP
    squared = wave_a * wave_a + wave_b * wave_b + wave_c * wave_c
    smooth = jnp.where(
        squared > 0, jnp.exp(-0.5 * squared) / jnp.where(squared > 0, squared, 1.0), 0.0
    )
    smooth = jnp.concatenate([smooth, smooth], axis=0)
    smooth = jnp.concatenate([smooth, smooth], axis=1)

    def back_x(filtered, part, x1):
        for power in range(3):
            field = product(table(2 + power, pl.ds(H * x1, H)), filtered, ROW_COL)
            for s in range(2):
                if x1 == 0:
                    ref, row = send2[part], 2 * power + s
                else:
                    ref, row = send2[2 + power // 2], 4 * (power % 2) + 2 * part + s
                flat(ref)[pl.ds(row, H, stride=8), :] = field[:, H * s : H * s + H]

    kept = []
    for part in range(2):
        arrive(recv1, 4 * part, 4, part)
        pieces = []
        for n in range(4):
            pieces.append(
                jnp.concatenate(
                    [
                        flat(recv1)[pl.ds(8 * n + 4 * part + q, 32, stride=32), :]
                        for q in range(4)
                    ],
                    axis=0,
                )
            )
        plane = jnp.concatenate(
            [
                jnp.concatenate([piece[:, 64 * low : 64 * low + 64] for piece in pieces], axis=1)
                for low in range(2)
            ],
            axis=0,
        )
        along_x = product(table(1), split(plane), ROW_COL)
        along_y = product(split(along_x), table(0), ROW_ROW)
        filtered = split(along_y * smooth)
        kept.append(filtered)
        back_x(filtered, part, 0)
        swap(send2[part], recv2[part], 0, 6, 2 + part)
    for part in range(2):
        back_x(kept[part], part, 1)
    for power in range(3):
        swap(send2[2 + power // 2], recv2[2 + power // 2], 4 * (power % 2), 4, 4 + power)

    flip_lane = 1.0 - 2.0 * (lax.broadcasted_iota(jnp.int32, (1, N), 1) & 1).astype(F32)
    flip_line = 1.0 - 2.0 * (lax.broadcasted_iota(jnp.int32, (N, 1), 0) & 1).astype(F32)

    for x1 in range(2):
        if x1 == 0:
            arrive(recv2[0], 0, 6, 2)
            arrive(recv2[1], 0, 6, 3)
        shear = None
        for power in range(3):
            if x1 == 1:
                arrive(recv2[2 + power // 2], 4 * (power % 2), 4, 4 + power)
            halves = []
            for part in range(2):
                if x1 == 0:
                    ref, row = recv2[part], 2 * power
                else:
                    ref, row = recv2[2 + power // 2], 4 * (power % 2) + 2 * part
                halves.append(
                    jnp.concatenate(
                        [flat(ref)[pl.ds(row + s, H, stride=8), :] for s in range(2)], axis=1
                    )
                )
            held = split(jnp.concatenate(halves, axis=0))
            for first, second, weight in PAIRS:
                if first != power:
                    continue
                back_y = product(held, table(5 + second), ROW_ROW)
                tidal = product(table(5 + 2 - first - second), split(back_y), ROW_COL)
                term = weight * (tidal * tidal)
                shear = term if shear is None else shear + term
        turned = jnp.transpose(shear)
        lines = []
        for high in range(2):
            lines.append(product(split(turned), table(0), ROW_ROW))
            turned = turned * flip_lane
        lines = jnp.concatenate(lines, axis=1)
        for high in range(2):
            both = product(table(0), split(lines), ROW_COL)
            lines = lines * flip_line
            for side in range(2):
                cosine = both[:H, N * side : N * side + N]
                sine = both[H:, N * side : N * side + N]
                real_part = cosine[:, :H] - sine[:, H:]
                imag_part = -(cosine[:, H:] + sine[:, :H])
                for n in range(2):
                    here = slice(64 * n, 64 * n + 64)
                    send3[x1][H * high : H * high + H, pl.ds(N * side + H * n, H)] = (
                        jnp.concatenate([real_part[:, here], imag_part[:, here]], axis=1)
                    )

        def tile(place, x1=x1):
            return send3[x1].at[
                pl.ds(pl.multiple_of(place // 4 * 8, 8), 8),
                pl.ds(pl.multiple_of(place % 4 * H, H), H),
            ]

        exchange(tile, lambda place, x1=x1: recv3[x1].at[place], recv3[x1], 7 + x1)

    arrive(recv3[0], 0, 8, 7)
    arrive(recv3[1], 0, 8, 8)
    for wait in waits:
        wait.wait()

def finish(first, second, high, low, real_out, imag_out, *refs):
    final, store_sem = refs[:4], refs[4]
    me = lax.axis_index("wide") * 4 + lax.axis_index("narrow")
    recv3 = (first, second)

    def flat(ref):
        return ref.reshape(8 * NUM, H)

    line = lax.broadcasted_iota(jnp.int32, (H, H), 0)
    lane = lax.broadcasted_iota(jnp.int32, (H, H), 1)
    for b in range(8):
        plus = flat(recv3[0])[pl.ds(b, H, stride=8), :]
        minus = flat(recv3[1])[pl.ds(b, H, stride=8), :]
        even = jnp.where(line == 0, plus, plus + minus)
        odd = plus - minus
        swapped = pltpu.roll(odd, 64, 1)
        odd = jnp.where(line == 0, minus, jnp.where(lane < 64, swapped, -swapped))
        both = jnp.concatenate([even, odd], axis=0)
        done = product(split(jnp.transpose(both)), (high[...], low[...]), ROW_COL)
        real_part, imag_part = done[:64], done[64:]
        if b == 0:
            anchor = (
                (lax.broadcasted_iota(jnp.int32, (64, N), 0) == 0)
                & (lax.broadcasted_iota(jnp.int32, (64, N), 1) == 0)
                & (me == 0)
            )
            real_part = jnp.where(anchor, 0.0, real_part)
            imag_part = jnp.where(anchor, 0.0, imag_part)
        for part, value in enumerate((real_part, imag_part)):
            for side in range(2):
                final[2 * part + side][pl.ds(b, 64, stride=8), :] = value[
                    :, H * side : H * side + H
                ]
    stores = [
        pltpu.make_async_copy(
            final[2 * part + side],
            (real_out, imag_out)[part].at[:, pl.ds(H * side, H)],
            store_sem.at[2 * part + side],
        )
        for part in range(2)
        for side in range(2)
    ]
    for store in stores:
        store.start()
    for store in stores:
        store.wait()


def per_device(density):
    arrays = [jnp.asarray(table) for table in tables()]
    last = arrays[TABLES:]
    joined = jnp.asarray(np.concatenate(tables()[:TABLES]))
    buffer = pltpu.VMEM((NUM, 8, H), F32)
    held = pl.pallas_call(
        body,
        out_shape=(OUT, OUT),
        in_specs=[pl.BlockSpec(memory_space=pl.ANY)] * 2,
        out_specs=[pl.BlockSpec(memory_space=pltpu.VMEM)] * 2,
        scratch_shapes=[pltpu.VMEM((N, N), BF16)] * TABLES
        + [buffer] * 10
        + [pltpu.VMEM((N, 512), F32)] * 2
        + [
            pltpu.VMEM(density.shape, F32),
            pltpu.SemaphoreType.DMA,
            pltpu.SemaphoreType.DMA((TABLES,)),
            pltpu.SemaphoreType.DMA((PHASES,)),
            pltpu.SemaphoreType.DMA((PHASES,)),
        ],
        compiler_params=pltpu.CompilerParams(
            collective_id=0, has_side_effects=True, vmem_limit_bytes=55259955
        ),
        name="tidal",
    )(density, joined)
    result = jax.ShapeDtypeStruct((512, N), F32)
    real_part, imag_part = pl.pallas_call(
        finish,
        out_shape=(result, result),
        in_specs=[pl.BlockSpec(memory_space=pltpu.VMEM)] * 4,
        out_specs=[pl.BlockSpec(memory_space=pl.ANY)] * 2,
        scratch_shapes=[pltpu.VMEM((512, H), F32)] * 4 + [pltpu.SemaphoreType.DMA((4,))],
        compiler_params=pltpu.CompilerParams(vmem_limit_bytes=16 * 2**20),
        name="finish",
    )(*held, *last)
    return real_part.reshape(64, 8, N), imag_part.reshape(64, 8, N)


def solution(mesh):
    return jax.shard_map(
        per_device,
        mesh=mesh,
        in_specs=(P("wide", "narrow", None),),
        out_specs=(P("narrow", "wide", None), P("narrow", "wide", None)),
        check_vma=False,
    )
```

```python
import math
import random

import jax
import jax.numpy as jnp
import ml_dtypes
import numpy as np
from jax import lax
from jax.experimental import pallas as pl
from jax.experimental.pallas import tpu as pltpu
from jax.sharding import PartitionSpec as P

LOGICAL = pl.DeviceIdType.LOGICAL
BF16 = jnp.bfloat16
F32 = jnp.float32
N = 256
H = 128
STEP = 2.0 * math.pi / N
NUM = 128


def split_np(table):
    table = np.asarray(table, np.float32)
    high = table.astype(ml_dtypes.bfloat16)
    low = (table - high.astype(np.float32)).astype(ml_dtypes.bfloat16)
    return high, low


def angle(rows, cols):
    return (np.asarray(rows)[:, None] * np.asarray(cols)[None, :] % N) * STEP


def tables():
    half = np.arange(H)
    full = np.arange(N)
    slab = np.concatenate([half, [H], N - half[1:]])
    wave = half * STEP
    weight = np.where(half == 0, 1.0, 2.0) / N
    cos_sin = np.concatenate([np.cos(angle(half, full)), np.sin(angle(half, full))])

    def back(points, power):
        cosine = np.cos(angle(points, half)) * (weight * wave**power)
        sine = np.sin(angle(points, half)) * (weight * wave**power)
        if power == 1:
            return np.concatenate([sine, -cosine], axis=1)
        return np.concatenate([cosine, sine], axis=1)

    back_slab = [back(slab, power) for power in range(3)]
    back_full = [back(full, power) for power in range(3)]
    even = np.cos(angle(half, full))
    odd = np.sin(angle(half, full))
    odd[0] = np.where(full % 2 == 0, 1.0, -1.0)
    last_x = np.concatenate([even, odd]) / float(N) ** 1.5
    order = (
        np.arange(2)[:, None, None]
        + 2 * np.arange(4)[None, :, None]
        + 8 * np.arange(32)[None, None, :]
    ).reshape(-1)
    out = []
    for table in [cos_sin, cos_sin[:, order]] + back_slab + back_full + [last_x]:
        out += list(split_np(table))
    return out


def split(value):
    high = value.astype(BF16)
    low = (value - high.astype(F32)).astype(BF16)
    return high, low


def product(left, right, dims):
    def one(a, b):
        return lax.dot_general(a, b, (dims, ((), ())), preferred_element_type=F32)

    return one(left[0], right[0]) + (one(left[0], right[1]) + one(left[1], right[0]))


ROW_COL = ((1,), (0,))
ROW_ROW = ((1,), (1,))
PAIRS = ((0, 0, 1.0), (0, 1, 2.0), (0, 2, 1.0), (1, 0, 2.0), (1, 1, 2.0), (2, 0, 1.0))


def hops(offset):
    return sum(min(step, 4 - step) for step in offset[:3])


def order():
    offsets = [
        (x, y, z, core)
        for x in range(4)
        for y in range(4)
        for z in range(4)
        for core in range(2)
        if x + y + z + core > 0
    ]
    random.Random(1).shuffle(offsets)
    return sorted(offsets, key=lambda offset: hops(offset) < 4)


ORDER = order()


def places(wide, narrow):
    x, y = lax.rem(wide, 4), lax.rem(lax.div(wide, 4), 4)
    z = 2 * lax.div(wide, 16) + lax.div(narrow, 2)
    core = lax.rem(narrow, 2)
    along_x = [4 * lax.rem(x + step, 4) for step in range(4)]
    along_y = [16 * lax.rem(y + step, 4) for step in range(4)]
    along_z = []
    for step in range(4):
        there = lax.rem(z + step, 4)
        along_z.append(64 * lax.div(there, 2) + 2 * lax.rem(there, 2))
    cores = [core, 1 - core]
    return [along_x[a] + along_y[b] + along_z[c] + cores[d] for a, b, c, d in ORDER]


def walk(me, visit):
    def step(_, place):
        place = place + 37
        place = jnp.where(place >= NUM, place - NUM, place)
        visit(place)
        return place

    lax.fori_loop(1, NUM, step, me, unroll=8)


TABLES = 16
OUT = jax.ShapeDtypeStruct((NUM, 8, H), F32)
PHASES = 9
DISTANT_FIRST = (0, 1, 5, 6, 8)


def body(density, *refs):
    consts, refs = refs[0], refs[1:]
    recv3, refs = refs[:2], refs[2:]
    tabs, refs = refs[:TABLES], refs[TABLES:]
    send1, recv1 = refs[0], refs[1]
    send2, recv2 = refs[2:6], refs[6:10]
    send3 = refs[10:12]
    field, field_sem, load_sem, sent, got = refs[12:]
    wide = lax.axis_index("wide")
    narrow = lax.axis_index("narrow")
    me = wide * 4 + narrow

    fetch = pltpu.make_async_copy(density, field, field_sem)
    fetch.start()
    barrier = pltpu.get_barrier_semaphore()

    def greet(place):
        pl.semaphore_signal(barrier, inc=1, device_id=place, device_id_type=LOGICAL)

    others = places(wide, narrow)
    walk(me, greet)
    loads = [
        pltpu.make_async_copy(consts.at[pl.ds(N * i, N)], tabs[i], load_sem.at[i])
        for i in range(TABLES)
    ]
    for load in loads:
        load.start()

    def table(number, *index):
        return tabs[2 * number][index or ...], tabs[2 * number + 1][index or ...]

    def ready(number):
        loads[2 * number].wait()
        loads[2 * number + 1].wait()

    waits = []

    def exchange(source, target, whole, phase):
        pltpu.make_async_copy(source(me), target(me), got.at[phase]).start()

        def start(place):
            pltpu.make_async_remote_copy(
                src_ref=source(place),
                dst_ref=target(me),
                send_sem=sent.at[phase],
                recv_sem=got.at[phase],
                device_id=place,
                device_id_type=LOGICAL,
            ).start()

        if phase in DISTANT_FIRST:
            for place in others:
                start(place)
        else:
            walk(me, start)
        part = whole.at[pl.ds(0, NUM - 1)]
        waits.append(pltpu.make_async_copy(part, part, sent.at[phase]))

    def swap(send, recv, first, count, phase):
        exchange(
            lambda place: send.at[place, pl.ds(first, count)],
            lambda place: recv.at[place, pl.ds(first, count)],
            send.at[:, pl.ds(first, count)],
            phase,
        )

    def arrive(recv, first, count, phase):
        part = recv.at[:, pl.ds(first, count)]
        pltpu.make_async_copy(part, part, got.at[phase]).wait()

    def flat(ref):
        return ref.reshape(8 * NUM, H)

    ready(0)
    fetch.wait()
    block = split(field[...].reshape(512, N))
    for part in range(2):
        lines = product(table(0, pl.ds(H * part, H)), block, ROW_ROW)
        for q in range(4):
            flat(send1)[pl.ds(4 * part + q, H, stride=8), :] = lines[:, H * q : H * q + H]
        if part == 0:
            pl.semaphore_wait(barrier, NUM - 1)
        swap(send1, recv1, 4 * part, 4, part)

    for number in range(1, TABLES // 2):
        ready(number)
    wave_a = lax.broadcasted_iota(jnp.int32, (H, H), 0).astype(F32) * STEP
    wave_b = lax.broadcasted_iota(jnp.int32, (H, H), 1).astype(F32) * STEP
    wave_c = me.astype(F32) * STEP
    squared = wave_a * wave_a + wave_b * wave_b + wave_c * wave_c
    smooth = jnp.where(
        squared > 0, jnp.exp(-0.5 * squared) / jnp.where(squared > 0, squared, 1.0), 0.0
    )
    smooth = jnp.concatenate([smooth, smooth], axis=0)
    smooth = jnp.concatenate([smooth, smooth], axis=1)

    def back_x(filtered, part, x1):
        for power in range(3):
            field = product(table(2 + power, pl.ds(H * x1, H)), filtered, ROW_COL)
            for s in range(2):
                if x1 == 0:
                    ref, row = send2[part], 2 * power + s
                else:
                    ref, row = send2[2 + power // 2], 4 * (power % 2) + 2 * part + s
                flat(ref)[pl.ds(row, H, stride=8), :] = field[:, H * s : H * s + H]

    kept = []
    for part in range(2):
        arrive(recv1, 4 * part, 4, part)
        pieces = []
        for n in range(4):
            pieces.append(
                jnp.concatenate(
                    [
                        flat(recv1)[pl.ds(8 * n + 4 * part + q, 32, stride=32), :]
                        for q in range(4)
                    ],
                    axis=0,
                )
            )
        plane = jnp.concatenate(
            [
                jnp.concatenate([piece[:, 64 * low : 64 * low + 64] for piece in pieces], axis=1)
                for low in range(2)
            ],
            axis=0,
        )
        along_x = product(table(1), split(plane), ROW_COL)
        along_y = product(split(along_x), table(0), ROW_ROW)
        filtered = split(along_y * smooth)
        kept.append(filtered)
        back_x(filtered, part, 0)
        swap(send2[part], recv2[part], 0, 6, 2 + part)
    for part in range(2):
        back_x(kept[part], part, 1)
    for power in range(3):
        swap(send2[2 + power // 2], recv2[2 + power // 2], 4 * (power % 2), 4, 4 + power)

    flip_lane = 1.0 - 2.0 * (lax.broadcasted_iota(jnp.int32, (1, N), 1) & 1).astype(F32)
    flip_line = 1.0 - 2.0 * (lax.broadcasted_iota(jnp.int32, (N, 1), 0) & 1).astype(F32)

    for x1 in range(2):
        if x1 == 0:
            arrive(recv2[0], 0, 6, 2)
            arrive(recv2[1], 0, 6, 3)
        shear = None
        for power in range(3):
            if x1 == 1:
                arrive(recv2[2 + power // 2], 4 * (power % 2), 4, 4 + power)
            halves = []
            for part in range(2):
                if x1 == 0:
                    ref, row = recv2[part], 2 * power
                else:
                    ref, row = recv2[2 + power // 2], 4 * (power % 2) + 2 * part
                halves.append(
                    jnp.concatenate(
                        [flat(ref)[pl.ds(row + s, H, stride=8), :] for s in range(2)], axis=1
                    )
                )
            held = split(jnp.concatenate(halves, axis=0))
            for first, second, weight in PAIRS:
                if first != power:
                    continue
                back_y = product(held, table(5 + second), ROW_ROW)
                tidal = product(table(5 + 2 - first - second), split(back_y), ROW_COL)
                term = weight * (tidal * tidal)
                shear = term if shear is None else shear + term
        turned = jnp.transpose(shear)
        lines = []
        for high in range(2):
            lines.append(product(split(turned), table(0), ROW_ROW))
            turned = turned * flip_lane
        lines = jnp.concatenate(lines, axis=1)
        for high in range(2):
            both = product(table(0), split(lines), ROW_COL)
            lines = lines * flip_line
            for side in range(2):
                cosine = both[:H, N * side : N * side + N]
                sine = both[H:, N * side : N * side + N]
                real_part = cosine[:, :H] - sine[:, H:]
                imag_part = -(cosine[:, H:] + sine[:, :H])
                for n in range(2):
                    here = slice(64 * n, 64 * n + 64)
                    send3[x1][H * high : H * high + H, pl.ds(N * side + H * n, H)] = (
                        jnp.concatenate([real_part[:, here], imag_part[:, here]], axis=1)
                    )

        def tile(place, x1=x1):
            return send3[x1].at[
                pl.ds(pl.multiple_of(place // 4 * 8, 8), 8),
                pl.ds(pl.multiple_of(place % 4 * H, H), H),
            ]

        exchange(tile, lambda place, x1=x1: recv3[x1].at[place], recv3[x1], 7 + x1)

    arrive(recv3[0], 0, 8, 7)
    arrive(recv3[1], 0, 8, 8)
    for wait in waits:
        wait.wait()

def finish(first, second, high, low, real_out, imag_out, *refs):
    final, store_sem = refs[:4], refs[4]
    me = lax.axis_index("wide") * 4 + lax.axis_index("narrow")
    recv3 = (first, second)

    def flat(ref):
        return ref.reshape(8 * NUM, H)

    line = lax.broadcasted_iota(jnp.int32, (H, H), 0)
    lane = lax.broadcasted_iota(jnp.int32, (H, H), 1)
    for b in range(8):
        plus = flat(recv3[0])[pl.ds(b, H, stride=8), :]
        minus = flat(recv3[1])[pl.ds(b, H, stride=8), :]
        even = jnp.where(line == 0, plus, plus + minus)
        odd = plus - minus
        swapped = pltpu.roll(odd, 64, 1)
        odd = jnp.where(line == 0, minus, jnp.where(lane < 64, swapped, -swapped))
        both = jnp.concatenate([even, odd], axis=0)
        done = product(split(jnp.transpose(both)), (high[...], low[...]), ROW_COL)
        real_part, imag_part = done[:64], done[64:]
        if b == 0:
            anchor = (
                (lax.broadcasted_iota(jnp.int32, (64, N), 0) == 0)
                & (lax.broadcasted_iota(jnp.int32, (64, N), 1) == 0)
                & (me == 0)
            )
            real_part = jnp.where(anchor, 0.0, real_part)
            imag_part = jnp.where(anchor, 0.0, imag_part)
        for part, value in enumerate((real_part, imag_part)):
            for side in range(2):
                final[2 * part + side][pl.ds(b, 64, stride=8), :] = value[
                    :, H * side : H * side + H
                ]
    stores = [
        pltpu.make_async_copy(
            final[2 * part + side],
            (real_out, imag_out)[part].at[:, pl.ds(H * side, H)],
            store_sem.at[2 * part + side],
        )
        for part in range(2)
        for side in range(2)
    ]
    for store in stores:
        store.start()
    for store in stores:
        store.wait()


def per_device(density):
    arrays = [jnp.asarray(table) for table in tables()]
    last = arrays[TABLES:]
    joined = jnp.asarray(np.concatenate(tables()[:TABLES]))
    buffer = pltpu.VMEM((NUM, 8, H), F32)
    held = pl.pallas_call(
        body,
        out_shape=(OUT, OUT),
        in_specs=[pl.BlockSpec(memory_space=pl.ANY)] * 2,
        out_specs=[pl.BlockSpec(memory_space=pltpu.VMEM)] * 2,
        scratch_shapes=[pltpu.VMEM((N, N), BF16)] * TABLES
        + [buffer] * 10
        + [pltpu.VMEM((N, 512), F32)] * 2
        + [
            pltpu.VMEM(density.shape, F32),
            pltpu.SemaphoreType.DMA,
            pltpu.SemaphoreType.DMA((TABLES,)),
            pltpu.SemaphoreType.DMA((PHASES,)),
            pltpu.SemaphoreType.DMA((PHASES,)),
        ],
        compiler_params=pltpu.CompilerParams(
            collective_id=0, has_side_effects=True, vmem_limit_bytes=55259955
        ),
        name="tidal",
    )(density, joined)
    result = jax.ShapeDtypeStruct((512, N), F32)
    real_part, imag_part = pl.pallas_call(
        finish,
        out_shape=(result, result),
        in_specs=[pl.BlockSpec(memory_space=pltpu.VMEM)] * 4,
        out_specs=[pl.BlockSpec(memory_space=pl.ANY)] * 2,
        scratch_shapes=[pltpu.VMEM((512, H), F32)] * 4 + [pltpu.SemaphoreType.DMA((4,))],
        compiler_params=pltpu.CompilerParams(vmem_limit_bytes=16 * 2**20),
        name="finish",
    )(*held, *last)
    return real_part.reshape(64, 8, N), imag_part.reshape(64, 8, N)


def solution(mesh):
    return jax.shard_map(
        per_device,
        mesh=mesh,
        in_specs=(P("wide", "narrow", None),),
        out_specs=(P("narrow", "wide", None), P("narrow", "wide", None)),
        check_vma=False,
    )
```

```python
import math
import random

import jax
import jax.numpy as jnp
import ml_dtypes
import numpy as np
from jax import lax
from jax.experimental import pallas as pl
from jax.experimental.pallas import tpu as pltpu
from jax.sharding import PartitionSpec as P

LOGICAL = pl.DeviceIdType.LOGICAL
BF16 = jnp.bfloat16
F32 = jnp.float32
N = 256
H = 128
STEP = 2.0 * math.pi / N
NUM = 128


def split_np(table):
    table = np.asarray(table, np.float32)
    high = table.astype(ml_dtypes.bfloat16)
    low = (table - high.astype(np.float32)).astype(ml_dtypes.bfloat16)
    return high, low


def angle(rows, cols):
    return (np.asarray(rows)[:, None] * np.asarray(cols)[None, :] % N) * STEP


def tables():
    half = np.arange(H)
    full = np.arange(N)
    slab = np.concatenate([half, [H], N - half[1:]])
    wave = half * STEP
    weight = np.where(half == 0, 1.0, 2.0) / N
    cos_sin = np.concatenate([np.cos(angle(half, full)), np.sin(angle(half, full))])

    def back(points, power):
        cosine = np.cos(angle(points, half)) * (weight * wave**power)
        sine = np.sin(angle(points, half)) * (weight * wave**power)
        if power == 1:
            return np.concatenate([sine, -cosine], axis=1)
        return np.concatenate([cosine, sine], axis=1)

    back_slab = [back(slab, power) for power in range(3)]
    back_full = [back(full, power) for power in range(3)]
    even = np.cos(angle(half, full))
    odd = np.sin(angle(half, full))
    odd[0] = np.where(full % 2 == 0, 1.0, -1.0)
    last_x = np.concatenate([even, odd]) / float(N) ** 1.5
    order = (
        np.arange(2)[:, None, None]
        + 2 * np.arange(4)[None, :, None]
        + 8 * np.arange(32)[None, None, :]
    ).reshape(-1)
    out = []
    for table in [cos_sin, cos_sin[:, order]] + back_slab + back_full + [last_x]:
        out += list(split_np(table))
    return out


def split(value):
    high = value.astype(BF16)
    low = (value - high.astype(F32)).astype(BF16)
    return high, low


def product(left, right, dims):
    def one(a, b):
        return lax.dot_general(a, b, (dims, ((), ())), preferred_element_type=F32)

    return one(left[0], right[0]) + (one(left[0], right[1]) + one(left[1], right[0]))


ROW_COL = ((1,), (0,))
ROW_ROW = ((1,), (1,))
PAIRS = ((0, 0, 1.0), (0, 1, 2.0), (0, 2, 1.0), (1, 0, 2.0), (1, 1, 2.0), (2, 0, 1.0))


def hops(offset):
    return sum(min(step, 4 - step) for step in offset[:3])


def order():
    offsets = [
        (x, y, z, core)
        for x in range(4)
        for y in range(4)
        for z in range(4)
        for core in range(2)
        if x + y + z + core > 0
    ]
    random.Random(1).shuffle(offsets)
    return sorted(offsets, key=lambda offset: -hops(offset))


ORDER = order()


def places(wide, narrow):
    x, y = lax.rem(wide, 4), lax.rem(lax.div(wide, 4), 4)
    z = 2 * lax.div(wide, 16) + lax.div(narrow, 2)
    core = lax.rem(narrow, 2)
    along_x = [4 * lax.rem(x + step, 4) for step in range(4)]
    along_y = [16 * lax.rem(y + step, 4) for step in range(4)]
    along_z = []
    for step in range(4):
        there = lax.rem(z + step, 4)
        along_z.append(64 * lax.div(there, 2) + 2 * lax.rem(there, 2))
    cores = [core, 1 - core]
    return [along_x[a] + along_y[b] + along_z[c] + cores[d] for a, b, c, d in ORDER]


def walk(me, visit):
    def step(_, place):
        place = place + 37
        place = jnp.where(place >= NUM, place - NUM, place)
        visit(place)
        return place

    lax.fori_loop(1, NUM, step, me, unroll=8)


TABLES = 16
OUT = jax.ShapeDtypeStruct((NUM, 8, H), F32)
PHASES = 9
DISTANT_FIRST = (0, 6, 8)


def body(density, *refs):
    consts, refs = refs[0], refs[1:]
    recv3, refs = refs[:2], refs[2:]
    tabs, refs = refs[:TABLES], refs[TABLES:]
    send1, recv1 = refs[0], refs[1]
    send2, recv2 = refs[2:6], refs[6:10]
    send3 = refs[10:12]
    field, field_sem, load_sem, sent, got = refs[12:]
    wide = lax.axis_index("wide")
    narrow = lax.axis_index("narrow")
    me = wide * 4 + narrow

    fetch = pltpu.make_async_copy(density, field, field_sem)
    fetch.start()
    loads = [
        pltpu.make_async_copy(consts.at[pl.ds(N * i, N)], tabs[i], load_sem.at[i])
        for i in range(TABLES)
    ]
    for load in loads[:2]:
        load.start()
    barrier = pltpu.get_barrier_semaphore()

    def greet(place):
        pl.semaphore_signal(barrier, inc=1, device_id=place, device_id_type=LOGICAL)

    others = places(wide, narrow)
    for place in others:
        greet(place)
    for load in loads[2:]:
        load.start()

    def table(number, *index):
        return tabs[2 * number][index or ...], tabs[2 * number + 1][index or ...]

    def ready(number):
        loads[2 * number].wait()
        loads[2 * number + 1].wait()

    waits = []

    def exchange(source, target, whole, phase):
        pltpu.make_async_copy(source(me), target(me), got.at[phase]).start()

        def start(place):
            pltpu.make_async_remote_copy(
                src_ref=source(place),
                dst_ref=target(me),
                send_sem=sent.at[phase],
                recv_sem=got.at[phase],
                device_id=place,
                device_id_type=LOGICAL,
            ).start()

        if phase in DISTANT_FIRST:
            for place in others:
                start(place)
        else:
            walk(me, start)
        part = whole.at[pl.ds(0, NUM - 1)]
        waits.append(pltpu.make_async_copy(part, part, sent.at[phase]))

    def swap(send, recv, first, count, phase):
        exchange(
            lambda place: send.at[place, pl.ds(first, count)],
            lambda place: recv.at[place, pl.ds(first, count)],
            send.at[:, pl.ds(first, count)],
            phase,
        )

    def arrive(recv, first, count, phase):
        part = recv.at[:, pl.ds(first, count)]
        pltpu.make_async_copy(part, part, got.at[phase]).wait()

    def flat(ref):
        return ref.reshape(8 * NUM, H)

    ready(0)
    fetch.wait()
    block = split(field[...].reshape(512, N))
    for part in range(2):
        lines = product(table(0, pl.ds(H * part, H)), block, ROW_ROW)
        for q in range(4):
            flat(send1)[pl.ds(4 * part + q, H, stride=8), :] = lines[:, H * q : H * q + H]
        if part == 0:
            pl.semaphore_wait(barrier, NUM - 1)
        swap(send1, recv1, 4 * part, 4, part)

    for number in range(1, TABLES // 2):
        ready(number)
    wave_a = lax.broadcasted_iota(jnp.int32, (H, H), 0).astype(F32) * STEP
    wave_b = lax.broadcasted_iota(jnp.int32, (H, H), 1).astype(F32) * STEP
    wave_c = me.astype(F32) * STEP
    squared = wave_a * wave_a + wave_b * wave_b + wave_c * wave_c
    smooth = jnp.where(
        squared > 0, jnp.exp(-0.5 * squared) / jnp.where(squared > 0, squared, 1.0), 0.0
    )
    smooth = jnp.concatenate([smooth, smooth], axis=0)
    smooth = jnp.concatenate([smooth, smooth], axis=1)

    def back_x(filtered, part, x1):
        for power in range(3):
            field = product(table(2 + power, pl.ds(H * x1, H)), filtered, ROW_COL)
            for s in range(2):
                if x1 == 0:
                    ref, row = send2[part], 2 * power + s
                else:
                    ref, row = send2[2 + power // 2], 4 * (power % 2) + 2 * part + s
                flat(ref)[pl.ds(row, H, stride=8), :] = field[:, H * s : H * s + H]

    kept = []
    for part in range(2):
        arrive(recv1, 4 * part, 4, part)
        pieces = []
        for n in range(4):
            pieces.append(
                jnp.concatenate(
                    [
                        flat(recv1)[pl.ds(8 * n + 4 * part + q, 32, stride=32), :]
                        for q in range(4)
                    ],
                    axis=0,
                )
            )
        plane = jnp.concatenate(
            [
                jnp.concatenate([piece[:, 64 * low : 64 * low + 64] for piece in pieces], axis=1)
                for low in range(2)
            ],
            axis=0,
        )
        along_x = product(table(1), split(plane), ROW_COL)
        along_y = product(split(along_x), table(0), ROW_ROW)
        filtered = split(along_y * smooth)
        kept.append(filtered)
        back_x(filtered, part, 0)
        swap(send2[part], recv2[part], 0, 6, 2 + part)
    for part in range(2):
        back_x(kept[part], part, 1)
    for power in range(3):
        swap(send2[2 + power // 2], recv2[2 + power // 2], 4 * (power % 2), 4, 4 + power)

    flip_lane = 1.0 - 2.0 * (lax.broadcasted_iota(jnp.int32, (1, N), 1) & 1).astype(F32)
    flip_line = 1.0 - 2.0 * (lax.broadcasted_iota(jnp.int32, (N, 1), 0) & 1).astype(F32)

    for x1 in range(2):
        if x1 == 0:
            arrive(recv2[0], 0, 6, 2)
            arrive(recv2[1], 0, 6, 3)
        shear = None
        for power in range(3):
            if x1 == 1:
                arrive(recv2[2 + power // 2], 4 * (power % 2), 4, 4 + power)
            halves = []
            for part in range(2):
                if x1 == 0:
                    ref, row = recv2[part], 2 * power
                else:
                    ref, row = recv2[2 + power // 2], 4 * (power % 2) + 2 * part
                halves.append(
                    jnp.concatenate(
                        [flat(ref)[pl.ds(row + s, H, stride=8), :] for s in range(2)], axis=1
                    )
                )
            held = split(jnp.concatenate(halves, axis=0))
            for first, second, weight in PAIRS:
                if first != power:
                    continue
                back_y = product(held, table(5 + second), ROW_ROW)
                tidal = product(table(5 + 2 - first - second), split(back_y), ROW_COL)
                term = weight * (tidal * tidal)
                shear = term if shear is None else shear + term
        turned = jnp.transpose(shear)
        lines = []
        for high in range(2):
            lines.append(product(split(turned), table(0), ROW_ROW))
            turned = turned * flip_lane
        lines = jnp.concatenate(lines, axis=1)
        for high in range(2):
            both = product(table(0), split(lines), ROW_COL)
            lines = lines * flip_line
            for side in range(2):
                cosine = both[:H, N * side : N * side + N]
                sine = both[H:, N * side : N * side + N]
                real_part = cosine[:, :H] - sine[:, H:]
                imag_part = -(cosine[:, H:] + sine[:, :H])
                for n in range(2):
                    here = slice(64 * n, 64 * n + 64)
                    send3[x1][H * high : H * high + H, pl.ds(N * side + H * n, H)] = (
                        jnp.concatenate([real_part[:, here], imag_part[:, here]], axis=1)
                    )

        def tile(place, x1=x1):
            return send3[x1].at[
                pl.ds(pl.multiple_of(place // 4 * 8, 8), 8),
                pl.ds(pl.multiple_of(place % 4 * H, H), H),
            ]

        exchange(tile, lambda place, x1=x1: recv3[x1].at[place], recv3[x1], 7 + x1)

    arrive(recv3[0], 0, 8, 7)
    arrive(recv3[1], 0, 8, 8)
    for wait in waits:
        wait.wait()

def finish(first, second, high, low, real_out, imag_out, *refs):
    final, store_sem = refs[:4], refs[4]
    me = lax.axis_index("wide") * 4 + lax.axis_index("narrow")
    recv3 = (first, second)

    def flat(ref):
        return ref.reshape(8 * NUM, H)

    line = lax.broadcasted_iota(jnp.int32, (H, H), 0)
    lane = lax.broadcasted_iota(jnp.int32, (H, H), 1)
    turned = []
    for b in range(8):
        plus = flat(recv3[0])[pl.ds(b, H, stride=8), :]
        minus = flat(recv3[1])[pl.ds(b, H, stride=8), :]
        even = jnp.where(line == 0, plus, plus + minus)
        odd = plus - minus
        swapped = pltpu.roll(odd, 64, 1)
        odd = jnp.where(line == 0, minus, jnp.where(lane < 64, swapped, -swapped))
        turned.append(jnp.transpose(jnp.concatenate([even, odd], axis=0)))
    anchor = (
        (lax.broadcasted_iota(jnp.int32, (32, N), 0) == 0)
        & (lax.broadcasted_iota(jnp.int32, (32, N), 1) == 0)
        & (me == 0)
    )
    stores = []
    for piece in range(2):
        for part in range(2):
            first = 64 * part + 32 * piece
            rows = jnp.concatenate([block[first : first + 32] for block in turned], axis=0)
            done = product(split(rows), (high[...], low[...]), ROW_COL)
            for b in range(8):
                value = done[32 * b : 32 * b + 32]
                if b == 0 and piece == 0:
                    value = jnp.where(anchor, 0.0, value)
                for side in range(2):
                    final[2 * part + side][pl.ds(N * piece + b, 32, stride=8), :] = value[
                        :, H * side : H * side + H
                    ]
            for side in range(2):
                store = pltpu.make_async_copy(
                    final[2 * part + side].at[pl.ds(N * piece, N)],
                    (real_out, imag_out)[part].at[pl.ds(N * piece, N), pl.ds(H * side, H)],
                    store_sem.at[len(stores)],
                )
                store.start()
                stores.append(store)
    for store in stores:
        store.wait()


def per_device(density):
    arrays = [jnp.asarray(table) for table in tables()]
    last = arrays[TABLES:]
    joined = jnp.asarray(np.concatenate(tables()[:TABLES]))
    buffer = pltpu.VMEM((NUM, 8, H), F32)
    held = pl.pallas_call(
        body,
        out_shape=(OUT, OUT),
        in_specs=[pl.BlockSpec(memory_space=pl.ANY)] * 2,
        out_specs=[pl.BlockSpec(memory_space=pltpu.VMEM)] * 2,
        scratch_shapes=[pltpu.VMEM((N, N), BF16)] * TABLES
        + [buffer] * 10
        + [pltpu.VMEM((N, 512), F32)] * 2
        + [
            pltpu.VMEM(density.shape, F32),
            pltpu.SemaphoreType.DMA,
            pltpu.SemaphoreType.DMA((TABLES,)),
            pltpu.SemaphoreType.DMA((PHASES,)),
            pltpu.SemaphoreType.DMA((PHASES,)),
        ],
        compiler_params=pltpu.CompilerParams(
            collective_id=0, has_side_effects=True, vmem_limit_bytes=55259955
        ),
        name="tidal",
    )(density, joined)
    result = jax.ShapeDtypeStruct((512, N), F32)
    real_part, imag_part = pl.pallas_call(
        finish,
        out_shape=(result, result),
        in_specs=[pl.BlockSpec(memory_space=pltpu.VMEM)] * 4,
        out_specs=[pl.BlockSpec(memory_space=pl.ANY)] * 2,
        scratch_shapes=[pltpu.VMEM((512, H), F32)] * 4 + [pltpu.SemaphoreType.DMA((8,))],
        compiler_params=pltpu.CompilerParams(vmem_limit_bytes=16 * 2**20),
        name="finish",
    )(*held, *last)
    return real_part.reshape(64, 8, N), imag_part.reshape(64, 8, N)


def solution(mesh):
    return jax.shard_map(
        per_device,
        mesh=mesh,
        in_specs=(P("wide", "narrow", None),),
        out_specs=(P("narrow", "wide", None), P("narrow", "wide", None)),
        check_vma=False,
    )
```
